32 devices in a mesh: fsdp: 4 (over y, x), ctx: 8 (over z, core).
Axes of the slice: x: 2, y: 2, z: 4, core: 2. Of those that a mesh axis runs over, the one named last changes fastest.
Arguments:
- inputs: bfloat16 [4096, 768], P(('fsdp', 'ctx')), may hold values from -6 to 6
- segments: int32 [4, 1024], P('fsdp'), may hold values from 0 to 7, as said below
- positions: int32 [4, 1024], P('fsdp', 'ctx'), may hold values from 0 to 383, as said below
- attention_norm_gain: bfloat16 [768], P(('fsdp', 'ctx')), may hold values from 0.5 to 1.5
- query_key_value_weight: bfloat16 [768, 2304], P(('fsdp', 'ctx')), may hold values from -2.7063294 to 2.7063294
- attention_output_weight: bfloat16 [768, 768], P(('fsdp', 'ctx')), may hold values from -4 to 4
- feedforward_norm_gain: bfloat16 [768], P(('fsdp', 'ctx')), may hold values from 0.5 to 1.5
- input_projection_weight: bfloat16 [768, 2304], P(('fsdp', 'ctx')), may hold values from -0.21875 to 0.21875
- down_projection_weight: bfloat16 [768, 1152], P(('fsdp', 'ctx')), may hold values from -0.25 to 0.25
- cotangent: bfloat16 [4096, 768], P(('fsdp', 'ctx')), may hold values from -6 to 6
Outputs:
- outputs: bfloat16 [4096, 768], P(('fsdp', 'ctx'))
- input_grad: bfloat16 [4096, 768], P(('fsdp', 'ctx'))
- attn_gain_grad: float32 [768], P(('fsdp', 'ctx'))
- qkv_weight_grad: float32 [768, 2304], P(('fsdp', 'ctx'))
- out_weight_grad: float32 [768, 768], P(('fsdp', 'ctx'))
- mlp_gain_grad: float32 [768], P(('fsdp', 'ctx'))
- in_weight_grad: float32 [768, 2304], P(('fsdp', 'ctx'))
- down_weight_grad: float32 [768, 1152], P(('fsdp', 'ctx'))
The draws below stay inside these ranges and needn't reach their ends.
Inputs may be any that keep to these rules, and one draw needn't show every extreme that they name: `segments`: each row is cut into documents of consecutive tokens, each of 1 to 384 tokens, whose numbers rise along the row; the first document is number 0 and the last is number 1024 / 128 - 1; one document of each row has exactly 384 tokens. `positions`: the position of each token within its document, counting from 0.
All inputs are finite; a program needn't handle non-finite values.
Results may differ from the reference program's by a relative error of at most 0.04.
Values may be sent and summed in bfloat16 or wider, within the bound.
No kernel may reach another device: no remote copies, remote signals or barrier semaphores. Data moves between devices by JAX's collectives and lax.ppermute only.
A program may use at most 128 MiB of HBM per device.

```python
import math
import jax
import jax.numpy as jnp
from jax import lax

MODEL_WIDTH = 768
HEAD = 64
FF = 1152
TOK_DEV = 128
ROWS = 4
PACKED_LENGTH = 1024
TOKENS = 4096
LONGEST_DOCUMENT = 384


def document_layout(key):
    row_keys = jax.random.split(jax.random.fold_in(key, 17), ROWS)
    length_count = PACKED_LENGTH // TOK_DEV
    choose_range = max(1, (length_count - 3) // 3)

    def single_packed_row(row_key):
        first_key, second_key = jax.random.split(row_key)
        lengths = jax.random.randint(first_key, (length_count,), TOK_DEV, 3 * TOK_DEV + 1).astype(jnp.int32)
        chosen = jax.random.randint(second_key, (), 0, choose_range)
        slot_ids = jnp.arange(length_count, dtype=jnp.int32)
        lengths = jnp.where(slot_ids == chosen, LONGEST_DOCUMENT, lengths).astype(jnp.int32)
        doc_ends = jnp.cumsum(lengths).astype(jnp.int32)
        doc_starts = doc_ends - lengths
        token_position_index = jnp.arange(PACKED_LENGTH, dtype=jnp.int32)
        segment = jnp.sum((token_position_index[:, None] >= doc_ends[None, :]).astype(jnp.int32), axis=1).astype(jnp.int32)
        onehot = segment[:, None] == slot_ids[None, :]
        offset = jnp.sum(jnp.where(onehot, doc_starts[None, :], 0), axis=1).astype(jnp.int32)
        final_segment = segment[PACKED_LENGTH - 1]
        numbered = jnp.where(segment == final_segment, length_count - 1, segment).astype(jnp.int32)
        return (numbered, (token_position_index - offset).astype(jnp.int32))
    return jax.vmap(single_packed_row)(row_keys)


def draw_segments(key, part):
    return document_layout(key)[0]


def draw_positions(key, part):
    return document_layout(key)[1]


def draw_query_key_value_weight(key, part):
    base = jax.random.truncated_normal(jax.random.fold_in(key, 5), -6.0, 6.0, (MODEL_WIDTH, 3 * MODEL_WIDTH), jnp.float32) * MODEL_WIDTH ** (-0.5)
    return base.astype(jnp.bfloat16)


def strengthened(result, own_key, source, target, blocks, factor):
    owner, partner = [(jnp.arange(result.shape[position]) // (result.shape[position] // blocks)).reshape([-1 if axis == position else 1 for axis in range(result.ndim)]) for position in (source, target)]
    chosen = jax.random.permutation(own_key, blocks)[partner]
    strong = (owner == chosen) | (owner == (partner + blocks // 2) % blocks)
    return jnp.where(strong, factor * result, result)


def levels(rng, dims, cuts, low, high):
    level, own = 1.0, jax.random.fold_in(rng, 6)
    for axis_at, parts in cuts:
        steps = jnp.exp(jax.random.uniform(jax.random.fold_in(own, axis_at), (parts,), jnp.float32, low / len(cuts), high / len(cuts)))
        level = level * jnp.repeat(steps, dims[axis_at] // parts).reshape([-1 if axis == axis_at else 1 for axis in range(len(dims))])
    return level


def scatter_about(rng, shape, scale, bound, cuts=(), kind=jnp.bfloat16):
    factor_of = levels(rng, shape, cuts, -0.22, 0.18) if cuts else 1.0
    values = jax.random.normal(rng, shape, jnp.float32) * scale * factor_of
    return jnp.minimum(jnp.maximum(values, -bound), bound).astype(kind)


def heavy_noise(own_key, dims, deviation, most, cuts, heavy, kind=jnp.bfloat16):
    entries = deviation * jax.random.normal(own_key, dims, jnp.float32)
    if cuts:
        entries = entries * levels(own_key, dims, cuts, -0.22, 0.18)
    return jnp.clip(strengthened(entries, jax.random.fold_in(own_key, 3), *heavy), -most, most).astype(kind)


def setup_inputs(seed: int = 0) -> dict:
    key_list = jax.random.split(jax.random.key(seed), 11)
    return {
        "inputs": scatter_about(key_list[0], (TOKENS, MODEL_WIDTH), 1.0, 6.0, ((0, 32),)),
        "segments": draw_segments(jax.random.fold_in(key_list[10], 71), 0),
        "positions": draw_positions(jax.random.fold_in(key_list[10], 71), 0),
        "attention_norm_gain": jnp.clip(1.0 + 0.1 * jax.random.normal(key_list[3], (MODEL_WIDTH,), jnp.float32), 0.5, 1.5).astype(jnp.bfloat16),
        "query_key_value_weight": draw_query_key_value_weight(jax.random.fold_in(key_list[10], 71), 0),
        "attention_output_weight": scatter_about(key_list[5], (MODEL_WIDTH, MODEL_WIDTH), (0.5 * (2 * TOK_DEV) ** 0.5 * MODEL_WIDTH ** -0.5), 4.0, ((0, 32),)),
        "feedforward_norm_gain": jnp.clip(1.0 + 0.1 * jax.random.normal(key_list[6], (MODEL_WIDTH,), jnp.float32), 0.5, 1.5).astype(jnp.bfloat16),
        "input_projection_weight": scatter_about(key_list[7], (MODEL_WIDTH, 2 * FF), MODEL_WIDTH ** -0.5, 0.21875, ((0, 32),)),
        "down_projection_weight": scatter_about(key_list[8], (MODEL_WIDTH, FF), (FF // 2) ** -0.5, 0.25, ((0, 32),)),
        "cotangent": heavy_noise(key_list[9], (TOKENS, MODEL_WIDTH), 1.0, 6.0, ((0, 32),), (0, 1, 32, 2.75)),
    }


THETA = 160000.0
EPS = 1e-05
NEG = -1e+30
SQRT_HALF = 0.7071067811865476
INV_SQRT_TAU = 0.3989422804014327

def layer_norm(values, gain):
    row_mean = lax.optimization_barrier(jnp.mean(values, axis=-1, keepdims=True))
    centred = values - row_mean
    variance = lax.optimization_barrier(jnp.mean(centred * centred, axis=-1, keepdims=True))
    inv_std = lax.rsqrt(variance + EPS)
    normed = centred * inv_std
    return (normed * gain, normed, inv_std)

def norm_back(grad_out, normed, inv_std, gain):
    grad_normed = grad_out * gain
    grad_gain = lax.optimization_barrier(jnp.sum(grad_out * normed, axis=0))
    first_mean = lax.optimization_barrier(jnp.mean(grad_normed, axis=-1, keepdims=True))
    second_mean = lax.optimization_barrier(jnp.mean(grad_normed * normed, axis=-1, keepdims=True))
    return (inv_std * (grad_normed - first_mean - normed * second_mean), grad_gain)

def gelu_parts(values):
    normal_cdf = 0.5 * (1.0 + lax.erf(values * SQRT_HALF))
    slope = normal_cdf + values * jnp.exp(-0.5 * values * values) * INV_SQRT_TAU
    return (values * normal_cdf, slope)

def rope_tables(where):
    half_dim = HEAD // 2
    freq = THETA ** (-(jnp.arange(half_dim).astype(jnp.float32) * (2.0 / HEAD)))
    angles = where.astype(jnp.float32)[:, None] * freq[None, :]
    cosine = jnp.cos(angles)
    sine = jnp.sin(angles)
    return (jnp.concatenate([cosine, cosine], -1)[:, None, :], jnp.concatenate([sine, sine], -1)[:, None, :])

def rotate(values, cosine, sine):
    half_dim = HEAD // 2
    turned = jnp.concatenate([-values[..., half_dim:], values[..., :half_dim]], -1)
    return values * cosine + turned * sine

def unrotate(grads, cosine, sine):
    half_dim = HEAD // 2
    scaled = grads * sine
    turned = jnp.concatenate([scaled[..., half_dim:], -scaled[..., :half_dim]], -1)
    return grads * cosine + turned

def to_low(values):
    return lax.optimization_barrier(values.astype(jnp.bfloat16)).astype(jnp.float32)

def single_packed_row(inputs, row_seg, row_pos, attention_norm_gain, query_key_value_weight, attention_output_weight, feedforward_norm_gain, input_projection_weight, down_projection_weight, cotangent):
    row_len = inputs.shape[0]
    heads = MODEL_WIDTH // HEAD
    scale_factor = HEAD ** (-0.5)
    x_float = inputs.astype(jnp.float32)
    attn_gain_f = attention_norm_gain.astype(jnp.float32)
    mlp_gain_f = feedforward_norm_gain.astype(jnp.float32)
    attn_scaled, attn_normed, attn_inv = layer_norm(x_float, attn_gain_f)
    attn_input = attn_scaled.astype(jnp.bfloat16)
    qkv_rows = jnp.dot(attn_input, query_key_value_weight, preferred_element_type=jnp.float32)
    cosine, sine = rope_tables(row_pos)
    query = rotate(qkv_rows[:, :MODEL_WIDTH].reshape(row_len, heads, HEAD), cosine, sine).astype(jnp.bfloat16)
    keys = rotate(qkv_rows[:, MODEL_WIDTH:2 * MODEL_WIDTH].reshape(row_len, heads, HEAD), cosine, sine).astype(jnp.bfloat16)
    values = qkv_rows[:, 2 * MODEL_WIDTH:].reshape(row_len, heads, HEAD).astype(jnp.bfloat16)
    key_float = keys.astype(jnp.float32)
    value_float = values.astype(jnp.float32)
    block = math.gcd(row_len, 256)
    blocks = row_len // block
    query_blocks = query.reshape(blocks, block, heads, HEAD)
    seg_blocks = row_seg.reshape(blocks, block)

    def scores_of(query_blk, seg_blk):
        scores = jnp.einsum('qhd,khd->hqk', query_blk.astype(jnp.float32), key_float) * scale_factor
        allowed = (seg_blk[:, None] == row_seg[None, :])[None]
        return (jnp.where(allowed, scores, NEG), allowed)

    def forward_block(carry, pieces):
        query_blk, seg_blk = pieces
        scores, allowed = scores_of(query_blk, seg_blk)
        top_score = lax.optimization_barrier(jnp.max(scores, axis=-1, keepdims=True))
        expd = jnp.where(allowed, jnp.exp(scores - top_score), 0.0)
        total = lax.optimization_barrier(jnp.sum(expd, axis=-1))
        weighted = jnp.einsum('hqk,khd->qhd', to_low(expd), value_float)
        attn_blk = (weighted / jnp.transpose(total)[:, :, None]).astype(jnp.bfloat16)
        lse_blk = top_score[..., 0] + jnp.log(total)
        return (carry, (attn_blk, lse_blk))
    unused, (attn_parts, lse_parts) = lax.scan(forward_block, jnp.zeros((), jnp.float32), (query_blocks, seg_blocks))
    attn_vec = attn_parts.reshape(row_len, MODEL_WIDTH)
    attn_proj = jnp.dot(attn_vec, attention_output_weight, preferred_element_type=jnp.float32)
    resid = x_float + attn_proj
    mlp_scaled, mlp_normed, mlp_inv = layer_norm(resid, mlp_gain_f)
    mlp_input = mlp_scaled.astype(jnp.bfloat16)
    up_rows = jnp.dot(mlp_input, input_projection_weight, preferred_element_type=jnp.float32)
    gate_in = up_rows[:, :FF]
    gate_mul = up_rows[:, FF:]
    gelu_value, gelu_slope = gelu_parts(gate_in)
    hidden = (gelu_value * gate_mul).astype(jnp.bfloat16)
    outputs = (resid + jnp.dot(hidden, down_projection_weight.T, preferred_element_type=jnp.float32)).astype(jnp.bfloat16)
    down_grad = jnp.dot(cotangent.T, hidden, preferred_element_type=jnp.float32)
    grad_hidden = jnp.dot(cotangent, down_projection_weight, preferred_element_type=jnp.float32)
    grad_up = jnp.concatenate([grad_hidden * gate_mul * gelu_slope, grad_hidden * gelu_value], axis=1).astype(jnp.bfloat16)
    in_grad = jnp.dot(mlp_input.T, grad_up, preferred_element_type=jnp.float32)
    grad_mlp_input = jnp.dot(grad_up, input_projection_weight.T, preferred_element_type=jnp.float32)
    grad_resid_n, mlp_gain_grad = norm_back(grad_mlp_input, mlp_normed, mlp_inv, mlp_gain_f)
    grad_resid = cotangent.astype(jnp.float32) + grad_resid_n
    grad_resid_low = grad_resid.astype(jnp.bfloat16)
    out_grad = jnp.dot(attn_vec.T, grad_resid_low, preferred_element_type=jnp.float32)
    grad_vec = jnp.dot(grad_resid_low, attention_output_weight.T, preferred_element_type=jnp.float32).astype(jnp.bfloat16)
    delta = lax.optimization_barrier(jnp.sum((grad_vec.astype(jnp.float32) * attn_vec.astype(jnp.float32)).reshape(row_len, heads, HEAD), axis=-1))
    grad_blocks = grad_vec.reshape(blocks, block, heads, HEAD)
    delta_blocks = delta.reshape(blocks, block, heads)

    def backward_block(carry, pieces):
        key_acc, value_acc = carry
        query_blk, seg_blk, grad_blk, lse_blk, delta_blk = pieces
        scores, allowed = scores_of(query_blk, seg_blk)
        probs = jnp.where(allowed, jnp.exp(scores - lse_blk[..., None]), 0.0)
        grad_float = grad_blk.astype(jnp.float32)
        value_acc = value_acc + jnp.einsum('hqk,qhd->khd', to_low(probs), grad_float)
        grad_probs = jnp.einsum('qhd,khd->hqk', grad_float, value_float)
        grad_scores = to_low(probs * (grad_probs - jnp.transpose(delta_blk)[:, :, None]) * scale_factor)
        grad_query = jnp.einsum('hqk,khd->qhd', grad_scores, key_float)
        key_acc = key_acc + jnp.einsum('hqk,qhd->khd', grad_scores, query_blk.astype(jnp.float32))
        return ((key_acc, value_acc), grad_query)
    zeros = jnp.zeros((row_len, heads, HEAD), jnp.float32)
    (key_grad, value_grad), query_parts = lax.scan(backward_block, (zeros, zeros), (query_blocks, seg_blocks, grad_blocks, lse_parts, delta_blocks))
    query_grad = query_parts.reshape(row_len, heads, HEAD)
    query_back = unrotate(query_grad, cosine, sine).reshape(row_len, MODEL_WIDTH)
    key_back = unrotate(key_grad, cosine, sine).reshape(row_len, MODEL_WIDTH)
    grad_qkv = jnp.concatenate([query_back, key_back, value_grad.reshape(row_len, MODEL_WIDTH)], axis=1).astype(jnp.bfloat16)
    qkv_grad = jnp.dot(attn_input.T, grad_qkv, preferred_element_type=jnp.float32)
    grad_attn_input = jnp.dot(grad_qkv, query_key_value_weight.T, preferred_element_type=jnp.float32)
    grad_x_n, attn_gain_grad = norm_back(grad_attn_input, attn_normed, attn_inv, attn_gain_f)
    input_grad = (grad_resid + grad_x_n).astype(jnp.bfloat16)
    return (outputs, input_grad, attn_gain_grad, qkv_grad, out_grad, mlp_gain_grad, in_grad, down_grad)

def reference(inputs, segments, positions, attention_norm_gain, query_key_value_weight, attention_output_weight, feedforward_norm_gain, input_projection_weight, down_projection_weight, cotangent):
    out_rows = []
    grad_rows = []
    sums = None
    for packed_row_index in range(ROWS):
        leading_entry = packed_row_index * PACKED_LENGTH
        collected_outputs = single_packed_row(inputs[leading_entry:leading_entry + PACKED_LENGTH], segments[packed_row_index], positions[packed_row_index], attention_norm_gain, query_key_value_weight, attention_output_weight, feedforward_norm_gain, input_projection_weight, down_projection_weight, cotangent[leading_entry:leading_entry + PACKED_LENGTH])
        out_rows.append(collected_outputs[0])
        grad_rows.append(collected_outputs[1])
        if sums is None:
            sums = list(collected_outputs[2:])
        else:
            sums = [held + fresh for held, fresh in zip(sums, collected_outputs[2:])]
    return (jnp.concatenate(out_rows, axis=0), jnp.concatenate(grad_rows, axis=0), sums[0], sums[1], sums[2], sums[3], sums[4], sums[5])
```

```python
import functools
import math

import jax
import jax.numpy as jnp
from jax import lax
from jax.experimental import pallas as pl
from jax.experimental.pallas import tpu as pltpu
from jax.sharding import PartitionSpec as P

HEAD = 64
FF = 1152
LONGEST_DOCUMENT = 384
LANES = 128
HEADS_STEP = 4
GROUP = HEADS_STEP * HEAD

THETA = 160000.0
EPS = 1e-05
NEG = -1e30
SQRT_HALF = 0.7071067811865476
INV_SQRT_TAU = 0.3989422804014327
AXES = ("fsdp", "ctx")
BF = jnp.bfloat16
F32 = jnp.float32


def exchange_groups(fsdp, ctx):
    bits = ctx.bit_length() - 1
    groups = []
    for low in range(1, bits, 2):
        high = min(low + 2, bits)
        groups.append([j << low for j in range(1 << (high - low))])
    groups.append([j * ctx for j in range(fsdp)])
    groups.append([0, 1])
    return groups


def slot_masks(groups):
    masks = [0]
    for group in groups:
        masks = [outer ^ inner for outer in group for inner in masks]
    return masks


def xor_permute(value, mask, count):
    return lax.ppermute(value, AXES, [(d, d ^ mask) for d in range(count)])


def gather_rows(shard, groups, count):
    held = shard
    for group in groups[:-1]:
        held = jnp.concatenate(
            [held] + [xor_permute(held, m, count) for m in group[1:]], axis=0
        )
    return held, xor_permute(held, groups[-1][1], count)


def scatter_rows(kept, sent, groups, count):
    held = kept + xor_permute(sent, groups[-1][1], count).astype(F32)
    for group in reversed(groups[:-1]):
        rows = held.shape[0] // len(group)
        total = held[:rows]
        for j, mask in enumerate(group):
            if j:
                part = held[j * rows : (j + 1) * rows].astype(BF)
                total = total + xor_permute(part, mask, count).astype(F32)
        held = total
    return held


def shifted(value, steps):
    ctx = lax.axis_size("ctx")
    first, last = max(0, -steps), min(ctx, ctx - steps)
    return lax.ppermute(value, "ctx", [(s, s + steps) for s in range(first, last)])


def dot(a, b):
    return jnp.dot(a, b, preferred_element_type=F32)


def dot_nt(a, b):
    return lax.dot_general(a, b, (((1,), (1,)), ((), ())), preferred_element_type=F32)


def dot_tn(a, b):
    return lax.dot_general(a, b, (((0,), (0,)), ((), ())), preferred_element_type=F32)


def layer_norm(values, gain):
    row_mean = jnp.mean(values, axis=-1, keepdims=True)
    centred = values - row_mean
    variance = jnp.mean(centred * centred, axis=-1, keepdims=True)
    inv_std = lax.rsqrt(variance + EPS)
    normed = centred * inv_std
    return (normed * gain, normed, inv_std)


def norm_back(grad_out, normed, inv_std, gain):
    grad_normed = grad_out * gain
    first_mean = jnp.mean(grad_normed, axis=-1, keepdims=True)
    second_mean = jnp.mean(grad_normed * normed, axis=-1, keepdims=True)
    return inv_std * (grad_normed - first_mean - normed * second_mean)


def gelu_parts(values):
    normal_cdf = 0.5 * (1.0 + lax.erf(values * SQRT_HALF))
    slope = normal_cdf + values * jnp.exp(-0.5 * values * values) * INV_SQRT_TAU
    return (values * normal_cdf, slope)


def rope_tables(where):
    lane = jnp.arange(LANES) % (HEAD // 2)
    freq = THETA ** (-(lane.astype(F32) * (2.0 / HEAD)))
    angles = where.astype(F32)[:, None] * freq[None, :]
    return jnp.cos(angles), jnp.sin(angles)


def half_sign(shape):
    lane = lax.broadcasted_iota(jnp.int32, shape, len(shape) - 1)
    return (lane % HEAD) < HEAD // 2


def swapped(values):
    half = HEAD // 2
    low = half_sign(values.shape)
    width = values.shape[-1]
    up = pltpu.roll(values, width - half, 1)
    down = pltpu.roll(values, half, 1)
    return low, jnp.where(low, up, down)


def rotate(values, cosine, sine):
    low, other = swapped(values)
    return values * cosine + jnp.where(low, -other, other) * sine


def unrotate(grads, cosine, sine):
    low, other = swapped(grads * sine)
    return grads * cosine + jnp.where(low, other, -other)


def wide(table):
    return jnp.concatenate([table] * (GROUP // LANES), axis=1)


def head_lanes(values, head):
    lane = lax.broadcasted_iota(jnp.int32, values.shape, 1)
    return jnp.where((lane // HEAD) == head, values, jnp.zeros_like(values))


def pick(first, second):
    lane = lax.broadcasted_iota(jnp.int32, first.shape, 1)
    return jnp.where(lane < HEAD, first, second)


def move_kernel(blocks, *refs):
    parts, table, out = refs[:blocks], refs[blocks], refs[blocks + 1]
    rows = parts[0].shape[0]
    for i in range(blocks):
        out[i * rows : (i + 1) * rows, :] = dot(parts[i][...], table[...]).astype(BF)


def forward_kernel(
    reach, x_ref, gain_ref, cos_ref, sin_ref, bias_ref,
    qa, qb, ka, kb, va, vb,
    q_out, k_out, v_out, attn_out, lse_out, norm_ref,
):
    tok = attn_out.shape[0]
    blocks = x_ref.shape[0] // tok
    scale = HEAD ** (-0.5)

    @pl.when(pl.program_id(0) == 0)
    def _():
        for i in range(blocks):
            rows = pl.ds(i * tok, tok)
            scaled, _, _ = layer_norm(x_ref[rows, :].astype(F32), gain_ref[0:1, :])
            norm_ref[rows, :] = scaled.astype(BF)

    half = norm_ref.shape[1] // 2
    for i in range(blocks):
        rows = pl.ds(i * tok, tok)
        xa, xb = norm_ref[rows, :half], norm_ref[rows, half:]
        cosine, sine = wide(cos_ref[rows, :]), wide(sin_ref[rows, :])
        q_out[rows, :] = rotate(dot(xa, qa[...]) + dot(xb, qb[...]), cosine, sine).astype(BF)
        k_out[rows, :] = rotate(dot(xa, ka[...]) + dot(xb, kb[...]), cosine, sine).astype(BF)
        v_out[rows, :] = (dot(xa, va[...]) + dot(xb, vb[...])).astype(BF)

    bias = bias_ref[...]
    own = pl.ds(reach * tok, tok)
    for pair in range(GROUP // LANES):
        lanes = slice(pair * LANES, (pair + 1) * LANES)
        query, key, value = q_out[own, lanes], k_out[:, lanes], v_out[:, lanes]
        results, logs = [], []
        for head in range(2):
            scores = dot_nt(head_lanes(query, head), key) * scale + bias
            top = jnp.max(scores, axis=-1, keepdims=True)
            weights = jnp.exp(scores - top)
            total = jnp.sum(weights, axis=-1, keepdims=True)
            results.append(dot(weights.astype(BF), value) / total)
            logs.append(jnp.broadcast_to(top + jnp.log(total), (tok, LANES)))
        attn_out[:, lanes] = pick(*results).astype(BF)
        lse_out[:, lanes] = pick(*logs)


def query_kernel(
    q_ref, k_ref, v_ref, g_ref, a_ref, lse_ref, bias_ref, cos_ref, sin_ref, out_ref
):
    scale = HEAD ** (-0.5)
    bias = bias_ref[...]
    cosine, sine = cos_ref[...], sin_ref[...]
    for pair in range(GROUP // LANES):
        lanes = slice(pair * LANES, (pair + 1) * LANES)
        query, key, value = q_ref[:, lanes], k_ref[:, lanes], v_ref[:, lanes]
        grad = g_ref[:, lanes]
        product = grad.astype(F32) * a_ref[:, lanes].astype(F32)
        results = []
        for head in range(2):
            lse = lse_ref[:, pair * LANES + head * HEAD : pair * LANES + head * HEAD + 1]
            delta = jnp.sum(head_lanes(product, head), axis=-1, keepdims=True)
            scores = dot_nt(head_lanes(query, head), key) * scale + bias
            probs = jnp.exp(scores - lse)
            grad_probs = dot_nt(head_lanes(grad, head), value)
            grad_scores = (probs * (grad_probs - delta) * scale).astype(BF)
            results.append(dot(grad_scores, key))
        out_ref[:, lanes] = unrotate(pick(*results), cosine, sine).astype(BF)


def key_kernel(blocks, q_ref, k_ref, v_ref, lse_ref, delta_ref, bias_ref, cos_ref, sin_ref, *refs):
    grads, key_out, value_out = refs[:blocks], refs[blocks], refs[blocks + 1]
    scale = HEAD ** (-0.5)
    bias = bias_ref[...]
    cosine, sine = cos_ref[...], sin_ref[...]
    first = pl.program_id(0) * HEADS_STEP
    for pair in range(GROUP // LANES):
        lanes = slice(pair * LANES, (pair + 1) * LANES)
        query, key, value = q_ref[:, lanes], k_ref[:, lanes], v_ref[:, lanes]
        grad = jnp.concatenate([g[:, lanes] for g in grads], axis=0)
        key_parts, value_parts = [], []
        for head in range(2):
            row = first + (2 * pair + head)
            lse = lse_ref[pl.ds(row, 1), :]
            delta = delta_ref[pl.ds(row, 1), :]
            scores = dot_nt(head_lanes(key, head), query) * scale + bias
            probs = jnp.exp(scores - lse)
            value_parts.append(dot(probs.astype(BF), grad))
            grad_probs = dot_nt(head_lanes(value, head), grad)
            grad_scores = (probs * (grad_probs - delta) * scale).astype(BF)
            key_parts.append(dot(grad_scores, query))
        key_out[:, lanes] = unrotate(pick(*key_parts), cosine, sine).astype(BF)
        value_out[:, lanes] = pick(*value_parts).astype(BF)


def whole(shape):
    return pl.BlockSpec(shape, lambda p: (0,) * len(shape))


def columns(rows, offset=0, row_block=0):
    return pl.BlockSpec((rows, GROUP), lambda p: (row_block, offset + p))


def high_low(values, pieces):
    out = []
    for _ in range(pieces):
        high = lax.reduce_precision(values, 8, 7)
        out.append(high.astype(BF))
        values = values - high
    return out


def local(
    inputs,
    segments,
    positions,
    attention_norm_gain,
    query_key_value_weight,
    attention_output_weight,
    feedforward_norm_gain,
    input_projection_weight,
    down_projection_weight,
    cotangent,
):
    tok, width = inputs.shape
    heads = width // HEAD
    half = width // 2
    rows = query_key_value_weight.shape[0]
    fsdp, ctx = lax.axis_size("fsdp"), lax.axis_size("ctx")
    count = fsdp * ctx
    groups = exchange_groups(fsdp, ctx)
    own_index = lax.axis_index("ctx")
    me = lax.axis_index("fsdp") * ctx + own_index
    reach = -(-LONGEST_DOCUMENT // tok)
    blocks = 2 * reach + 1
    window = blocks * tok
    steps = width // GROUP

    lane_id = jnp.arange(LANES)[None, :]
    gain_cols = jnp.where(
        lane_id == 0, attention_norm_gain[:, None], feedforward_norm_gain[:, None]
    )
    qkv_a, qkv_b = gather_rows(
        jnp.concatenate([query_key_value_weight, gain_cols], axis=1), groups, count
    )
    x_blocks = [inputs if r == 0 else shifted(inputs, -r) for r in range(-reach, reach + 1)]
    rest_a, rest_b = gather_rows(
        jnp.concatenate(
            [attention_output_weight, input_projection_weight, down_projection_weight], axis=1
        ),
        groups,
        count,
    )

    masks = jnp.asarray(slot_masks(groups), jnp.int32)
    source = ((me ^ masks)[:, None] * rows + jnp.arange(rows)[None, :]).reshape(-1)
    to_rel = (jnp.arange(width)[:, None] == source[None, :]).astype(BF)
    to_nat = (source[:, None] == jnp.arange(width)[None, :]).astype(BF)

    row_segs = segments[0]
    pad = reach * tok
    low_pad = jnp.full((pad,), -1, jnp.int32)
    high_pad = jnp.full((pad,), jnp.iinfo(jnp.int32).max, jnp.int32)
    window_segs = lax.dynamic_slice_in_dim(
        jnp.concatenate([low_pad, row_segs, high_pad]), own_index * tok, window
    )
    own_segs = window_segs[pad : pad + tok]
    before = jnp.sum((window_segs[None, :] < window_segs[:, None]).astype(jnp.int32), axis=1)
    cosine, sine = rope_tables(jnp.arange(window) - before)
    bias = jnp.where(own_segs[:, None] == window_segs[None, :], 0.0, NEG).astype(F32)

    cot_rel = dot(cotangent, to_rel).astype(BF)
    x_rel = pl.pallas_call(
        functools.partial(move_kernel, blocks),
        out_shape=jax.ShapeDtypeStruct((window, width), BF),
        name="move_inputs",
    )(*x_blocks, to_rel)

    gain_table = jnp.concatenate([qkv_a[:, 3 * width :], qkv_b[:, 3 * width :]], axis=0)
    select = (jnp.arange(8)[:, None] == jnp.arange(LANES)[None, :]).astype(BF)
    gains = dot_nt(select, gain_table)
    attn_gain, mlp_gain = gains[0:1], gains[1:2]

    window_cols = jax.ShapeDtypeStruct((window, width), BF)
    q_win, k_win, v_win, attn, lse = pl.pallas_call(
        functools.partial(forward_kernel, reach),
        grid=(steps,),
        in_specs=[
            whole((window, width)),
            whole((8, width)),
            whole((window, LANES)),
            whole((window, LANES)),
            whole((tok, window)),
            columns(half),
            columns(half),
            columns(half, steps),
            columns(half, steps),
            columns(half, 2 * steps),
            columns(half, 2 * steps),
        ],
        out_specs=[columns(window)] * 3 + [columns(tok)] * 2,
        out_shape=[window_cols] * 3
        + [jax.ShapeDtypeStruct((tok, width), BF), jax.ShapeDtypeStruct((tok, width), F32)],
        scratch_shapes=[pltpu.VMEM((window, width), BF)],
        name="attention_forward",
    )(x_rel, gains, cosine, sine, bias, qkv_a, qkv_b, qkv_a, qkv_b, qkv_a, qkv_b)

    out_rows = dot(to_rel[:, :half], rest_a[:, :width]) + dot(to_rel[:, half:], rest_b[:, :width])
    out_weight = dot(out_rows.astype(BF), to_rel).astype(BF)
    in_a, in_b = rest_a[:, width : width + 2 * FF], rest_b[:, width : width + 2 * FF]
    down_a, down_b = rest_a[:, width + 2 * FF :], rest_b[:, width + 2 * FF :]

    x_own = x_rel[pad : pad + tok].astype(F32)
    resid = x_own + dot(attn, out_weight)
    mlp_scaled, mlp_normed, mlp_inv = layer_norm(resid, mlp_gain)
    mlp_input = mlp_scaled.astype(BF)
    up_rows = dot(mlp_input[:, :half], in_a) + dot(mlp_input[:, half:], in_b)
    gate_in, gate_mul = up_rows[:, :FF], up_rows[:, FF:]
    gelu_value, gelu_slope = gelu_parts(gate_in)
    hidden = (gelu_value * gate_mul).astype(BF)
    grad_hidden = dot(cot_rel[:, :half], down_a) + dot(cot_rel[:, half:], down_b)
    grad_up = jnp.concatenate(
        [grad_hidden * gate_mul * gelu_slope, grad_hidden * gelu_value], axis=1
    ).astype(BF)
    grad_mlp_input = jnp.concatenate([dot_nt(grad_up, in_a), dot_nt(grad_up, in_b)], axis=1)
    grad_resid = cot_rel.astype(F32) + norm_back(grad_mlp_input, mlp_normed, mlp_inv, mlp_gain)
    grad_low = grad_resid.astype(BF)
    grad_attn = dot_nt(grad_low, out_weight).astype(BF)

    member = (jnp.arange(width)[:, None] // HEAD == jnp.arange(LANES)[None, :]).astype(F32)
    delta = jnp.dot(
        grad_attn.astype(F32) * attn.astype(F32), member, precision=lax.Precision.HIGHEST
    )[:, :heads]
    lse_cols = lse.reshape(tok, heads, HEAD)[:, :, 0]
    stats = high_low(lse_cols, 3) + high_low(delta, 2)
    filler = jnp.zeros((tok, LANES - 5 * heads), BF)
    message = jnp.concatenate([grad_attn] + stats + [filler], axis=1)
    messages = [message if r == 0 else shifted(message, -r) for r in range(-reach, reach + 1)]

    own_cols = columns(tok, 0, reach)
    table_own = pl.BlockSpec((tok, LANES), lambda p: (reach, 0))
    grad_query = pl.pallas_call(
        query_kernel,
        grid=(steps,),
        in_specs=[
            own_cols,
            columns(window),
            columns(window),
            columns(tok),
            columns(tok),
            columns(tok),
            whole((tok, window)),
            pl.BlockSpec((tok, LANES), lambda p: (reach, 0)),
            table_own,
        ],
        out_specs=columns(tok),
        out_shape=jax.ShapeDtypeStruct((tok, width), BF),
        name="attention_query_grad",
    )(q_win, k_win, v_win, grad_attn, attn, lse, bias, cosine, sine)

    attn_rel = dot(attn, to_rel).astype(BF)
    grad_low_nat = dot(grad_low, to_nat).astype(BF)
    ones = jnp.ones((tok, LANES), BF)
    mlp_gain_terms = (grad_mlp_input * mlp_normed).astype(BF)

    def rest_half(cut):
        return jnp.concatenate(
            [
                dot_tn(attn_rel[:, cut], grad_low_nat),
                dot_tn(mlp_input[:, cut], grad_up),
                dot_tn(cot_rel[:, cut], hidden),
                dot_tn(mlp_gain_terms[:, cut], ones),
            ],
            axis=1,
        )

    first, second = slice(0, half), slice(half, width)
    rest_part = scatter_rows(rest_half(first), rest_half(second).astype(BF), groups, count)

    down_rel = jnp.concatenate([dot_nt(hidden, down_a), dot_nt(hidden, down_b)], axis=1)
    outputs = dot((resid + down_rel).astype(BF), to_nat).astype(BF)

    stat_rows = jnp.concatenate([m[:, width:] for m in messages], axis=0).astype(F32)
    lse_win = (
        stat_rows[:, :heads] + stat_rows[:, heads : 2 * heads] + stat_rows[:, 2 * heads : 3 * heads]
    )
    delta_win = stat_rows[:, 3 * heads : 4 * heads] + stat_rows[:, 4 * heads : 5 * heads]
    grad_key, grad_value = pl.pallas_call(
        functools.partial(key_kernel, blocks),
        grid=(steps,),
        in_specs=[
            columns(window),
            own_cols,
            own_cols,
            whole((heads, window)),
            whole((heads, window)),
            whole((tok, window)),
            table_own,
            table_own,
        ]
        + [columns(tok)] * blocks,
        out_specs=[columns(tok)] * 2,
        out_shape=[jax.ShapeDtypeStruct((tok, width), BF)] * 2,
        name="attention_key_grad",
    )(q_win, k_win, v_win, lse_win.T, delta_win.T, bias, cosine, sine, *messages)

    grad_qkv = jnp.concatenate([grad_query, grad_key, grad_value], axis=1)
    grad_attn_input = jnp.concatenate(
        [dot_nt(grad_qkv, qkv_a[:, : 3 * width]), dot_nt(grad_qkv, qkv_b[:, : 3 * width])], axis=1
    )
    attn_scaled, attn_normed, attn_inv = layer_norm(x_own, attn_gain)
    attn_input = attn_scaled.astype(BF)
    attn_gain_terms = (grad_attn_input * attn_normed).astype(BF)

    def qkv_half(cut):
        return jnp.concatenate(
            [dot_tn(attn_input[:, cut], grad_qkv), dot_tn(attn_gain_terms[:, cut], ones)], axis=1
        )

    qkv_part = scatter_rows(qkv_half(first), qkv_half(second).astype(BF), groups, count)
    grad_x = norm_back(grad_attn_input, attn_normed, attn_inv, attn_gain)
    input_grad = dot((grad_resid + grad_x).astype(BF), to_nat).astype(BF)

    return (
        outputs,
        input_grad,
        qkv_part[:, 3 * width],
        qkv_part[:, : 3 * width],
        rest_part[:, :width],
        rest_part[:, 3 * FF + width],
        rest_part[:, width : width + 2 * FF],
        rest_part[:, width + 2 * FF : width + 3 * FF],
    )


def solution(mesh):
    in_specs = (
        P(("fsdp", "ctx"), None),
        P("fsdp", None),
        P("fsdp", "ctx"),
        P(("fsdp", "ctx")),
        P(("fsdp", "ctx"), None),
        P(("fsdp", "ctx"), None),
        P(("fsdp", "ctx")),
        P(("fsdp", "ctx"), None),
        P(("fsdp", "ctx"), None),
        P(("fsdp", "ctx"), None),
    )
    out_specs = (
        P(("fsdp", "ctx"), None),
        P(("fsdp", "ctx"), None),
        P(("fsdp", "ctx")),
        P(("fsdp", "ctx"), None),
        P(("fsdp", "ctx"), None),
        P(("fsdp", "ctx")),
        P(("fsdp", "ctx"), None),
        P(("fsdp", "ctx"), None),
    )
    return jax.shard_map(local, mesh=mesh, in_specs=in_specs, out_specs=out_specs, check_vma=False)
```
